32 devices in a mesh: geom: 2 (over x), row: 8 (over z, y), col: 2 (over core).
Axes of the slice: x: 2, y: 2, z: 4, core: 2. Of those that a mesh axis runs over, the one named last changes fastest.
Arguments:
- matrix: bfloat16 [128, 8, 128, 128], P(('geom', 'row'), 'col'), parts along dimension 0, may hold values from -1.5 to 1.5
- columns: int32 [64, 8], P('row'), may hold values from -1 to 63, as said below
Outputs:
- purified: bfloat16 [128, 8, 128, 128], P(('geom', 'row'), 'col'), parts along dimension 0
The draws below stay inside these ranges and needn't reach their ends.
There are 2 independent parts, one for each index of `geom`. The reference program is written for one: setup_inputs(seed, part) draws one part's arguments, and reference() takes and returns one part's arrays. A program takes and returns all parts, laid end to end along the dimension named above; an argument that names none is the same for every part. Nothing has to cross between parts.
Inputs may be any that keep to these rules, and one draw needn't show every extreme that they name: In block row i the valid slots come first and slot 0 holds i; valid slots hold distinct columns (i + d) mod 64 with -4 <= d <= 4, and the others hold -1. A block row has 1 to 8 valid slots, and some block row has 8.
All inputs are finite; a program needn't handle non-finite values.
Results may differ from the reference program's by a relative error of at most 0.0049.
Values may be sent and summed in bfloat16 or wider, within the bound.
A program may use at most 64 MiB of HBM per device.

```python
import jax
import jax.numpy as jnp
from jax import lax

BS = 128
K = 8
BR_DEV = 8
REACH = 4
NB = 64


def draw_columns(key, part):
    window_span = 2 * REACH
    row_keys = jax.random.split(jax.random.fold_in(key, 11), NB)

    def one_row(row_key):
        shuffled = jax.random.permutation(row_key, window_span)
        return jnp.where(shuffled < REACH, shuffled - REACH, shuffled - REACH + 1)
    offsets = jax.vmap(one_row)(row_keys)[:, :K - 1].astype(jnp.int32)
    offsets = jnp.concatenate([jnp.zeros((NB, 1), jnp.int32), offsets], axis=1)
    density_level = jax.random.randint(jax.random.fold_in(key, 12), (NB // BR_DEV,), (K + 2) // 3, K + 1)
    jitter = jax.random.randint(jax.random.fold_in(key, 13), (NB,), 0, 2)
    counts = jnp.clip(jnp.repeat(density_level, BR_DEV) - jitter, 1, K)
    counts = counts.at[0].set(K)
    row_ids = jnp.arange(NB, dtype=jnp.int32)
    col_ids = (row_ids[:, None] + offsets) % NB
    slot_ids = jnp.arange(K, dtype=jnp.int32)
    return jnp.where(slot_ids[None, :] < counts[:, None], col_ids, -1).astype(jnp.int32)


def block_scale(stream_key, extent, pieces, low, top_value):
    def one(dim, blocks):
        steps = jax.random.uniform(jax.random.fold_in(jax.random.fold_in(stream_key, 6), dim), (blocks,), jnp.float32, low / len(pieces), top_value / len(pieces))
        return jnp.repeat(jnp.exp(steps), extent[dim] // blocks).reshape((-1,) + (1,) * (len(extent) - dim - 1))

    gain = one(*pieces[0])
    for cut in pieces[1:]:
        gain = gain * one(*cut)
    return gain


def bell_draw(stream_key, extent, deviation, most, cuts=(), kind=jnp.bfloat16):
    array = deviation * jax.random.normal(stream_key, extent, jnp.float32)
    if cuts:
        array = array * block_scale(stream_key, extent, cuts, -0.22, 0.18)
    return jnp.clip(array, -most, most).astype(kind)


def setup_inputs(seed: int = 0, part: int = 0) -> dict:
    key_list = jax.random.split(jax.random.key(seed), 3)
    part_splits = jax.random.split(jax.random.fold_in(key_list[2], part), 3)
    return {
        "matrix": bell_draw(part_splits[0], (NB, K, BS, BS), (2.0 / (3 * BS) ** 0.5), 1.5, ((0, 8), (1, 2))),
        "columns": draw_columns(jax.random.fold_in(key_list[2], 71), part),
    }


def restricted_product(left_blocks, right_blocks, columns):
    def one_row(inputs):
        left_row, col_row = inputs
        source = jnp.where(col_row >= 0, col_row, 0).astype(jnp.int32)
        right_rows = right_blocks[source].astype(jnp.float32)
        source_cols = columns[source]
        matches = (source_cols[:, None, :] == col_row[None, :, None]) & (col_row[:, None, None] >= 0) & (col_row[None, :, None] >= 0)
        picked = jnp.einsum('tsu,tuab->tsab', matches.astype(jnp.float32), right_rows)
        return jnp.einsum('tab,tsbc->sac', left_row.astype(jnp.float32), picked)
    return lax.map(one_row, (left_blocks, columns))


def reference(matrix, columns):
    valid_mask = (columns >= 0)[:, :, None, None]
    square = restricted_product(matrix, matrix, columns)
    square = jnp.where(valid_mask, square, jnp.float32(0.0)).astype(jnp.bfloat16)
    cube_sum = restricted_product(square, matrix, columns)
    result = 3.0 * square.astype(jnp.float32) - 2.0 * cube_sum
    return jnp.where(valid_mask, result, jnp.float32(0.0)).astype(jnp.bfloat16)
```

```python
import functools

import jax
import jax.numpy as jnp
from jax import lax
from jax.experimental import pallas as pl
from jax.experimental.pallas import tpu as pltpu
from jax.sharding import PartitionSpec as P

REACH = 4
MESH = pl.DeviceIdType.MESH


def kernel(
    rows, slots, bs,
    cols_ref, x_ref, o_ref,
    near0, near1, near2, near3, far, send0, send1, send2, send3, panel, square, result, outbox,
    local_sem, xsend_sem, xrecv_sem, hsend_sem, hrecv_sem, osend_sem, orecv_sem,
):
    half = rows // 2
    own = x_ref.shape[1]
    width = rows + REACH
    near = (near0, near1, near2, near3)
    packed = (send0, send1, send2, send3)
    q = lax.axis_index("col")
    r = lax.axis_index("row")
    devices = lax.axis_size("row")
    total = rows * devices
    sign = 1 - 2 * q
    facing = lax.rem(r + 2 * q - 1 + devices, devices)
    partner = {"col": 1 - q}
    neighbour = {"row": facing, "col": 1 - q}

    def true_row(m, core):
        return m + core * (rows - 1 - 2 * m)

    barrier = pltpu.get_barrier_semaphore()
    pl.semaphore_signal(barrier, inc=1, device_id=partner, device_id_type=MESH)
    pl.semaphore_signal(barrier, inc=1, device_id=neighbour, device_id_type=MESH)

    mine = pl.ds(q * own, own)
    loads = []
    for m in range(half):
        loads.append(
            pltpu.make_async_copy(x_ref.at[true_row(m, q)], near[m].at[mine], local_sem.at[m])
        )
    loads.append(
        pltpu.make_async_copy(
            x_ref.at[pl.ds((1 - q) * half, half)], far.at[:, mine], local_sem.at[half]
        )
    )
    for copy in loads:
        copy.start()

    offset = []
    for m in range(rows):
        i = true_row(m, q)
        row = []
        for k in range(slots):
            col = cols_ref[i, k]
            d = col - (r * rows + i)
            d = jnp.where(d > total // 2, d - total, d)
            d = jnp.where(d < -(total // 2), d + total, d)
            row.append(jnp.where(col >= 0, d * sign, 2 * total))
        offset.append(row)

    def slot_of(m, d):
        found = jnp.int32(slots)
        for k in range(slots):
            found = jnp.where(offset[m][k] == d, k, found)
        return found

    slot = [{d: slot_of(m, d) for d in range(-REACH, REACH + 1)} for m in range(rows)]

    zero = jnp.zeros((bs, bs), x_ref.dtype)
    for m in range(half):
        near[m][slots] = zero
    for f in range(rows - half):
        far[f, slots] = zero
    for m in range(half):
        result[m, width] = zero
    for j in range(width):
        m = j - REACH
        if m < 0:
            blank = range(rows + 1 + m, width)
        else:
            blank = [c for c in range(width) if not m <= c <= m + 2 * REACH]
        for c in blank:
            panel[j, :, c * bs : (c + 1) * bs] = zero

    pl.semaphore_wait(barrier, 2)

    swaps = []
    for m in range(half):
        swaps.append(
            pltpu.make_async_remote_copy(
                src_ref=x_ref.at[true_row(m, 1 - q)],
                dst_ref=near[m].at[mine],
                send_sem=xsend_sem.at[m],
                recv_sem=xrecv_sem.at[m],
                device_id=partner,
                device_id_type=MESH,
            )
        )
    swaps.append(
        pltpu.make_async_remote_copy(
            src_ref=x_ref.at[pl.ds(q * half, half)],
            dst_ref=far.at[:, mine],
            send_sem=xsend_sem.at[half],
            recv_sem=xrecv_sem.at[half],
            device_id=partner,
            device_id_type=MESH,
        )
    )
    for copy in swaps:
        copy.start()

    halos = []
    for m in range(half):
        count = rows - m
        halo = pltpu.make_async_remote_copy(
            src_ref=packed[m],
            dst_ref=panel.at[REACH - 1 - m, :, pl.ds(0, count * bs)],
            send_sem=hsend_sem.at[m],
            recv_sem=hrecv_sem.at[m],
            device_id=neighbour,
            device_id_type=MESH,
        )
        halos.append(halo)
        loads[m].wait()
        swaps[m].wait_recv()
        for n in range(count):
            d = (REACH - 1 - n) - m
            packed[m][:, n * bs : (n + 1) * bs] = near[m][slot[m][d]]
        for d in range(-REACH, REACH + 1):
            c = m + d + REACH
            panel[m + REACH, :, c * bs : (c + 1) * bs] = near[m][slot[m][d]]
        halo.start()

    loads[half].wait()
    swaps[half].wait_recv()
    for m in range(half, rows):
        f = true_row(m, q) - (1 - q) * half
        for d in range(-REACH, REACH + 1):
            c = m + d + REACH
            if c < width:
                panel[m + REACH, :, c * bs : (c + 1) * bs] = far[f, slot[m][d]]

    tile = 2 * bs

    def product(left, p, c):
        low, high = max(p, c - REACH // 2), min(p + REACH, c + REACH // 2) + 1
        a = left[:, :, low * tile : high * tile].reshape(2 * bs, (high - low) * tile)
        b = panel[2 * low : 2 * high, :, c * tile : (c + 1) * tile].reshape((high - low) * tile, tile)
        return jnp.dot(a, b, preferred_element_type=jnp.float32)

    sent = []
    for p in reversed(range(half // 2)):
        for m in ((0, 1) if p else (2, 3)):
            halos[m].wait_recv()
        first = 2 * p
        for c in range(p, p + REACH + 1):
            value = product(panel.at[first + REACH : first + REACH + 2], p, c)
            for e in range(2):
                for g in range(2):
                    m = first + e
                    d = 2 * c + g - REACH - m
                    if -REACH <= d <= REACH:
                        keep = jnp.where(slot[m][d] == slots, 0.0, 1.0).astype(jnp.float32)
                        block = value[e * bs : (e + 1) * bs, g * bs : (g + 1) * bs] * keep
                        block = block.astype(jnp.bfloat16)
                    else:
                        block = zero
                    at = (2 * c + g) * bs
                    square[m, :, at : at + bs] = block
        for c in range(p, p + REACH + 1):
            value = product(square.at[first : first + 2], p, c)
            for e in range(2):
                for g in range(2):
                    m = first + e
                    at = (2 * c + g) * bs
                    cube = value[e * bs : (e + 1) * bs, g * bs : (g + 1) * bs]
                    whole = 3.0 * square[m, :, at : at + bs].astype(jnp.float32) - 2.0 * cube
                    result[m, 2 * c + g] = whole.astype(jnp.bfloat16)
        for m in (first, first + 1):
            i = true_row(m, q)
            for core in (1 - q, q):
                for s in range(own):
                    col = cols_ref[i, core * own + s]
                    d = col - (r * rows + i)
                    d = jnp.where(d > total // 2, d - total, d)
                    d = jnp.where(d < -(total // 2), d + total, d)
                    held = (col >= 0) & (d >= -REACH) & (d <= REACH)
                    at = jnp.where(held, d * sign + (m + REACH), width)
                    if core is q:
                        o_ref[i, s] = result[m, at]
                    else:
                        outbox[m, s] = result[m, at]
            copy = pltpu.make_async_remote_copy(
                src_ref=outbox.at[m],
                dst_ref=o_ref.at[i],
                send_sem=osend_sem.at[m],
                recv_sem=orecv_sem.at[m],
                device_id=partner,
                device_id_type=MESH,
            )
            copy.start()
            sent.append((m, copy))

    for copy in swaps + halos:
        copy.wait_send()
    for m, copy in sent:
        copy.wait_send()
        pltpu.make_async_remote_copy(
            src_ref=outbox.at[m],
            dst_ref=o_ref.at[true_row(m, 1 - q)],
            send_sem=osend_sem.at[m],
            recv_sem=orecv_sem.at[m],
            device_id=partner,
            device_id_type=MESH,
        ).wait_recv()


def local(matrix, columns):
    rows, own, bs = matrix.shape[0], matrix.shape[1], matrix.shape[2]
    slots = columns.shape[1]
    half = rows // 2
    width = rows + REACH
    kind = matrix.dtype
    dma = pltpu.SemaphoreType.DMA
    return pl.pallas_call(
        functools.partial(kernel, rows, slots, bs),
        out_shape=jax.ShapeDtypeStruct(matrix.shape, kind),
        in_specs=[
            pl.BlockSpec(memory_space=pltpu.SMEM),
            pl.BlockSpec(memory_space=pl.ANY),
        ],
        out_specs=pl.BlockSpec(memory_space=pltpu.VMEM),
        scratch_shapes=[pltpu.VMEM((slots + 1, bs, bs), kind)] * half
        + [pltpu.VMEM((rows - half, slots + 1, bs, bs), kind)]
        + [pltpu.VMEM((bs, (rows - m) * bs), kind) for m in range(half)]
        + [
            pltpu.VMEM((width, bs, width * bs), kind),
            pltpu.VMEM((half, bs, width * bs), kind),
            pltpu.VMEM((half, width + 1, bs, bs), kind),
            pltpu.VMEM((half, own, bs, bs), kind),
            dma((half + 1,)),
            dma((half + 1,)),
            dma((half + 1,)),
            dma((half,)),
            dma((half,)),
            dma((half,)),
            dma((half,)),
        ],
        compiler_params=pltpu.CompilerParams(
            collective_id=0, has_side_effects=True, vmem_limit_bytes=40 * 1024 * 1024
        ),
    )(columns, matrix)


def solution(mesh):
    placed = (P(("geom", "row"), "col", None, None), P("row", None))
    return jax.shard_map(
        local,
        mesh=mesh,
        in_specs=placed,
        out_specs=P(("geom", "row"), "col", None, None),
        check_vma=False,
    )
```

```python
import functools

import jax
import jax.numpy as jnp
from jax import lax
from jax.experimental import pallas as pl
from jax.experimental.pallas import tpu as pltpu
from jax.sharding import PartitionSpec as P

REACH = 4
MESH = pl.DeviceIdType.MESH


def kernel(
    rows, slots, bs,
    cols_hbm, x_ref, o_ref,
    near0, near1, near2, near3, far, send0, send1, send2, send3, panel, square, total, part, result,
    outbox, cols_ref,
    local_sem, cols_sem, xsend_sem, xrecv_sem, dsend_sem, drecv_sem, hsend_sem, hrecv_sem, osend_sem, orecv_sem,
):
    half = rows // 2
    own = x_ref.shape[1]
    width = rows + REACH
    near = (near0, near1, near2, near3)
    packed = (send0, send1, send2, send3)
    q = lax.axis_index("col")
    r = lax.axis_index("row")
    devices = lax.axis_size("row")
    count = rows * devices
    sign = 1 - 2 * q
    above = lax.rem(r + 1, devices)
    below = lax.rem(r - 1 + devices, devices)
    facing = lax.rem(r + 2 * q - 1 + devices, devices)
    partner = {"col": 1 - q}
    neighbour = {"row": facing, "col": 1 - q}

    def true_row(m, core):
        return m + core * (rows - 1 - 2 * m)

    barrier = pltpu.get_barrier_semaphore()
    pl.semaphore_signal(barrier, inc=1, device_id=neighbour, device_id_type=MESH)

    @pl.when(q == 0)
    def _():
        pl.semaphore_signal(barrier, inc=1, device_id={"row": below}, device_id_type=MESH)

    pl.semaphore_signal(barrier, inc=1, device_id=partner, device_id_type=MESH)

    table = pltpu.make_async_copy(cols_hbm, cols_ref, cols_sem)
    table.start()
    mine = pl.ds(q * own, own)
    loads = []
    for m in range(half):
        loads.append(
            pltpu.make_async_copy(x_ref.at[true_row(m, q)], near[m].at[mine], local_sem.at[m])
        )
    loads.append(
        pltpu.make_async_copy(
            x_ref.at[pl.ds((1 - q) * half, half)], far.at[:, mine], local_sem.at[half]
        )
    )
    for copy in loads:
        copy.start()

    def diagonal(m, core, to):
        at = REACH - 1 - m
        return pltpu.make_async_remote_copy(
            src_ref=x_ref.at[true_row(m, core), 0],
            dst_ref=panel.at[at, :, pl.ds(at * bs, bs)],
            send_sem=dsend_sem.at[core, m],
            recv_sem=drecv_sem.at[m],
            device_id=to,
            device_id_type=MESH,
        )

    down = [diagonal(m, 0, {"row": below, "col": 1}) for m in range(half)]
    up = [diagonal(m, 1, {"row": above, "col": 0}) for m in range(half)]

    swaps = []
    for m in range(half):
        swaps.append(
            pltpu.make_async_remote_copy(
                src_ref=x_ref.at[true_row(m, 1 - q)],
                dst_ref=near[m].at[mine],
                send_sem=xsend_sem.at[m],
                recv_sem=xrecv_sem.at[m],
                device_id=partner,
                device_id_type=MESH,
            )
        )
    swaps.append(
        pltpu.make_async_remote_copy(
            src_ref=x_ref.at[pl.ds(q * half, half)],
            dst_ref=far.at[:, mine],
            send_sem=xsend_sem.at[half],
            recv_sem=xrecv_sem.at[half],
            device_id=partner,
            device_id_type=MESH,
        )
    )

    zero = jnp.zeros((bs, bs), x_ref.dtype)
    for m in range(half):
        near[m][slots] = zero
    for f in range(rows - half):
        far[f, slots] = zero
    for m in range(half):
        result[m, width] = zero
    for j in range(width):
        m = j - REACH
        if m < 0:
            blank = range(rows + 1 + m, width)
        else:
            blank = [c for c in range(width) if not m <= c <= m + 2 * REACH]
        for c in blank:
            panel[j, :, c * bs : (c + 1) * bs] = zero

    pl.semaphore_wait(barrier, 3 - q)
    for copy in swaps[:half]:
        copy.start()

    @pl.when(q == 0)
    def _():
        for pair in zip(down, up):
            for copy in pair:
                copy.start()

    swaps[half].start()
    table.wait()

    def offset_of(i, k):
        col = cols_ref[i, k]
        d = col - (r * rows + i)
        d = jnp.where(d > count // 2, d - count, d)
        d = jnp.where(d < -(count // 2), d + count, d)
        return jnp.where(col >= 0, d * sign, 2 * count)

    offset = [[offset_of(true_row(m, q), k) for k in range(slots)] for m in range(rows)]

    def slot_of(m, d):
        found = jnp.int32(slots)
        for k in range(slots):
            found = jnp.where(offset[m][k] == d, k, found)
        return found

    slot = [{d: slot_of(m, d) for d in range(-REACH, REACH + 1)} for m in range(rows)]

    halos, pieces = [], []
    for m in range(half):
        middle, end = REACH - 1 - m, rows - m
        spans = [(middle + 1, end)] + ([(0, middle)] if middle else [])
        copies = []
        for low, high in spans:
            at = len(pieces)
            piece = pltpu.make_async_remote_copy(
                src_ref=packed[m].at[:, pl.ds(low * bs, (high - low) * bs)],
                dst_ref=panel.at[middle, :, pl.ds(low * bs, (high - low) * bs)],
                send_sem=hsend_sem.at[at],
                recv_sem=hrecv_sem.at[at],
                device_id=neighbour,
                device_id_type=MESH,
            )
            copies.append(piece)
            pieces.append(piece)
        halos.append(copies)
        loads[m].wait()
        swaps[m].wait_recv()
        for n in range(end):
            if n != middle:
                packed[m][:, n * bs : (n + 1) * bs] = near[m][slot[m][middle - n]]
        for d in range(-REACH, REACH + 1):
            c = m + d + REACH
            panel[m + REACH, :, c * bs : (c + 1) * bs] = near[m][slot[m][d]]
        for copy in copies:
            copy.start()

    loads[half].wait()
    swaps[half].wait_recv()
    for m in range(half, rows):
        f = true_row(m, q) - (1 - q) * half
        for d in range(-REACH, REACH + 1):
            c = m + d + REACH
            if c < width:
                panel[m + REACH, :, c * bs : (c + 1) * bs] = far[f, slot[m][d]]

    tile = 2 * bs

    def span(c):
        return slice(c * tile, (c + 1) * tile)

    def product(left, row, n, low, high, c):
        a = left[row : row + n, :, low * bs : high * bs].reshape(n * bs, (high - low) * bs)
        b = panel[low:high, :, span(c)].reshape((high - low) * bs, tile)
        out = jnp.dot(a, b, preferred_element_type=jnp.float32)
        return out.reshape(n, bs, tile)

    def reached(p, c):
        return 2 * max(p, c - REACH // 2), 2 * min(p + REACH, c + REACH // 2) + 2

    def finish_square(m, c):
        for g in range(2):
            at = 2 * c + g
            d = at - REACH - m
            if -REACH <= d <= REACH:
                keep = jnp.where(slot[m][d] == slots, 0.0, 1.0).astype(jnp.float32)
                block = (total[m, :, at * bs : (at + 1) * bs] * keep).astype(jnp.bfloat16)
            else:
                block = zero
            square[m, :, at * bs : (at + 1) * bs] = block

    def finish_cube(m, c, value):
        for g in range(2):
            at = 2 * c + g
            whole = 3.0 * square[m, :, at * bs : (at + 1) * bs].astype(jnp.float32)
            whole = whole - 2.0 * value[:, g * bs : (g + 1) * bs]
            result[m, at] = whole.astype(jnp.bfloat16)

    sent = []

    def hand_out(m):
        i = true_row(m, q)
        for core in (1 - q, q):
            for s in range(own):
                d = offset_of(i, core * own + s)
                at = jnp.where((d >= -REACH) & (d <= REACH), d + (m + REACH), width)
                if core is q:
                    o_ref[i, s] = result[m, at]
                else:
                    outbox[m, s] = result[m, at]
        copy = pltpu.make_async_remote_copy(
            src_ref=outbox.at[m],
            dst_ref=o_ref.at[i],
            send_sem=osend_sem.at[m],
            recv_sem=orecv_sem.at[m],
            device_id=partner,
            device_id_type=MESH,
        )
        copy.start()
        sent.append((m, copy))

    def arrive(m):
        down[m].wait_recv()
        for copy in halos[m]:
            copy.wait_recv()

    for p in range(half // 2):
        for c in range(p, p + REACH + 1):
            low, high = reached(p, c)
            total[2 * p : 2 * p + 2, :, span(c)] = product(
                panel, 2 * p + REACH, 2, max(low, REACH), high, c
            )
    arrive(0)
    arrive(1)
    for p in (1, 0):
        for c in range(p, REACH):
            total[2 * p : 2 * p + 2, :, span(c)] += product(
                panel, 2 * p + REACH, 2, REACH - 2, REACH, c
            )
        if p:
            for c in range(p, p + REACH + 1):
                finish_square(2, c)
                finish_square(3, c)
            for c in range(p, p + REACH + 1):
                low, high = reached(p, c)
                value = product(square, 2, 2, low, high, c)
                finish_cube(2, c, value[0])
                finish_cube(3, c, value[1])
            hand_out(2)
            hand_out(3)
    arrive(2)
    for c in range(3):
        total[0:2, :, span(c)] += product(panel, REACH, 2, 1, 2, c)
    for c in range(REACH + 1):
        finish_square(1, c)
    for c in range(REACH + 1):
        low, high = reached(0, c)
        finish_cube(1, c, product(square, 1, 1, max(low, 1), high, c)[0])
    hand_out(1)
    for c in (3, 4):
        finish_square(0, c)
    for c in range(1, REACH + 1):
        part[:, span(c)] = product(square, 0, 1, 6, reached(0, c)[1], c)[0]
    arrive(3)
    for c in range(3):
        total[0:1, :, span(c)] += product(panel, REACH, 1, 0, 1, c)
        finish_square(0, c)
    for c in range(REACH + 1):
        value = product(square, 0, 1, reached(0, c)[0], 6, c)[0]
        if c:
            value = value + part[:, span(c)]
        finish_cube(0, c, value)
    hand_out(0)

    for copy in swaps + pieces:
        copy.wait_send()

    @pl.when(q == 0)
    def _():
        for copy in down + up:
            copy.wait_send()

    for m, copy in sent:
        copy.wait_send()
        pltpu.make_async_remote_copy(
            src_ref=outbox.at[m],
            dst_ref=o_ref.at[true_row(m, 1 - q)],
            send_sem=osend_sem.at[m],
            recv_sem=orecv_sem.at[m],
            device_id=partner,
            device_id_type=MESH,
        ).wait_recv()


def local(matrix, columns):
    rows, own, bs = matrix.shape[0], matrix.shape[1], matrix.shape[2]
    slots = columns.shape[1]
    half = rows // 2
    assert rows == 2 * REACH and lax.axis_size("col") == 2
    width = rows + REACH
    kind = matrix.dtype
    dma = pltpu.SemaphoreType.DMA
    return pl.pallas_call(
        functools.partial(kernel, rows, slots, bs),
        out_shape=jax.ShapeDtypeStruct(matrix.shape, kind),
        in_specs=[
            pl.BlockSpec(memory_space=pltpu.HBM),
            pl.BlockSpec(memory_space=pltpu.HBM),
        ],
        out_specs=pl.BlockSpec(memory_space=pltpu.VMEM),
        scratch_shapes=[pltpu.VMEM((slots + 1, bs, bs), kind)] * half
        + [pltpu.VMEM((rows - half, slots + 1, bs, bs), kind)]
        + [pltpu.VMEM((bs, (rows - m) * bs), kind) for m in range(half)]
        + [
            pltpu.VMEM((width, bs, width * bs), kind),
            pltpu.VMEM((half, bs, width * bs), kind),
            pltpu.VMEM((half, bs, width * bs), jnp.float32),
            pltpu.VMEM((bs, width * bs), jnp.float32),
            pltpu.VMEM((half, width + 1, bs, bs), kind),
            pltpu.VMEM((half, own, bs, bs), kind),
            pltpu.SMEM(columns.shape, columns.dtype),
            dma((half + 1,)),
            dma,
            dma((half + 1,)),
            dma((half + 1,)),
            dma((2, half)),
            dma((half,)),
            dma((2 * half - 1,)),
            dma((2 * half - 1,)),
            dma((half,)),
            dma((half,)),
        ],
        compiler_params=pltpu.CompilerParams(
            collective_id=0, has_side_effects=True, vmem_limit_bytes=40 * 1024 * 1024
        ),
    )(
        pltpu.with_memory_space_constraint(columns, pltpu.HBM),
        pltpu.with_memory_space_constraint(matrix, pltpu.HBM),
    )


def solution(mesh):
    placed = (P(("geom", "row"), "col", None, None), P("row", None))
    return jax.shard_map(
        local,
        mesh=mesh,
        in_specs=placed,
        out_specs=P(("geom", "row"), "col", None, None),
        check_vma=False,
    )
```

```python
import functools

import jax
import jax.numpy as jnp
from jax import lax
from jax.experimental import pallas as pl
from jax.experimental.pallas import tpu as pltpu
from jax.sharding import PartitionSpec as P

REACH = 4
MESH = pl.DeviceIdType.MESH


def kernel(
    rows, slots, bs,
    cols_hbm, x_ref, o_ref,
    near0, near1, near2, near3, far, send0, send1, send2, send3, panel, square, total, part, result,
    outbox, cols_ref,
    local_sem, cols_sem, xsend_sem, xrecv_sem, dsend_sem, drecv_sem, hsend_sem, hrecv_sem, osend_sem, orecv_sem,
):
    half = rows // 2
    own = x_ref.shape[1]
    width = rows + REACH
    near = (near0, near1, near2, near3)
    packed = (send0, send1, send2, send3)
    q = lax.axis_index("col")
    r = lax.axis_index("row")
    devices = lax.axis_size("row")
    count = rows * devices
    sign = 1 - 2 * q
    facing = lax.rem(r + 2 * q - 1 + devices, devices)
    partner = {"col": 1 - q}
    neighbour = {"row": facing, "col": 1 - q}

    def true_row(m, core):
        return m + core * (rows - 1 - 2 * m)

    barrier = pltpu.get_barrier_semaphore()
    pl.semaphore_signal(barrier, inc=1, device_id=neighbour, device_id_type=MESH)

    pl.semaphore_signal(barrier, inc=1, device_id=partner, device_id_type=MESH)

    table = pltpu.make_async_copy(cols_hbm, cols_ref, cols_sem)
    table.start()
    mine = pl.ds(q * own, own)
    loads = []
    for m in range(half):
        loads.append(
            pltpu.make_async_copy(x_ref.at[true_row(m, q)], near[m].at[mine], local_sem.at[m])
        )
    loads.append(
        pltpu.make_async_copy(
            x_ref.at[pl.ds((1 - q) * half, half)], far.at[:, mine], local_sem.at[half]
        )
    )
    for copy in loads:
        copy.start()

    def diagonal(m, source):
        at = REACH - 1 - m
        return pltpu.make_async_remote_copy(
            src_ref=source,
            dst_ref=panel.at[at, :, pl.ds(at * bs, bs)],
            send_sem=dsend_sem.at[m],
            recv_sem=drecv_sem.at[m],
            device_id=neighbour,
            device_id_type=MESH,
        )

    held = [diagonal(m, x_ref.at[true_row(m, 0), 0]) for m in range(half)]
    passed = [diagonal(m, near[m].at[0]) for m in range(half)]

    swaps = []
    for m in range(half):
        swaps.append(
            pltpu.make_async_remote_copy(
                src_ref=x_ref.at[true_row(m, 1 - q)],
                dst_ref=near[m].at[mine],
                send_sem=xsend_sem.at[m],
                recv_sem=xrecv_sem.at[m],
                device_id=partner,
                device_id_type=MESH,
            )
        )
    swaps.append(
        pltpu.make_async_remote_copy(
            src_ref=x_ref.at[pl.ds(q * half, half)],
            dst_ref=far.at[:, mine],
            send_sem=xsend_sem.at[half],
            recv_sem=xrecv_sem.at[half],
            device_id=partner,
            device_id_type=MESH,
        )
    )

    zero = jnp.zeros((bs, bs), x_ref.dtype)
    for m in range(half):
        near[m][slots] = zero
    for f in range(rows - half):
        far[f, slots] = zero
    for m in range(half):
        result[m, width] = zero
    for j in range(width):
        m = j - REACH
        if m < 0:
            blank = range(rows + 1 + m, width)
        else:
            blank = [c for c in range(width) if not m <= c <= m + 2 * REACH]
        for c in blank:
            panel[j, :, c * bs : (c + 1) * bs] = zero

    pl.semaphore_wait(barrier, 2)
    for copy in swaps[:half]:
        copy.start()

    @pl.when(q == 0)
    def _():
        for copy in held:
            copy.start()

    swaps[half].start()
    table.wait()

    def offset_of(i, k):
        col = cols_ref[i, k]
        d = col - (r * rows + i)
        d = jnp.where(d > count // 2, d - count, d)
        d = jnp.where(d < -(count // 2), d + count, d)
        return jnp.where(col >= 0, d * sign, 2 * count)

    offset = [[offset_of(true_row(m, q), k) for k in range(slots)] for m in range(rows)]

    def slot_of(m, d):
        found = jnp.int32(slots)
        for k in range(slots):
            found = jnp.where(offset[m][k] == d, k, found)
        return found

    slot = [{d: slot_of(m, d) for d in range(-REACH, REACH + 1)} for m in range(rows)]

    def home_of(m, k):
        d = offset_of(true_row(m, q), k)
        return jnp.where((d >= -REACH) & (d <= REACH), d + (m + REACH), width)

    home = [
        [[home_of(m, core * own + s) for s in range(own)] for core in (1 - q, q)]
        for m in range(half)
    ]

    halos, pieces = [], []
    for m in range(half):
        middle, end = REACH - 1 - m, rows - m
        spans = [(middle + 1, end)] + ([(0, middle)] if middle else [])
        copies = []
        for low, high in spans:
            at = len(pieces)
            piece = pltpu.make_async_remote_copy(
                src_ref=packed[m].at[:, pl.ds(low * bs, (high - low) * bs)],
                dst_ref=panel.at[middle, :, pl.ds(low * bs, (high - low) * bs)],
                send_sem=hsend_sem.at[at],
                recv_sem=hrecv_sem.at[at],
                device_id=neighbour,
                device_id_type=MESH,
            )
            copies.append(piece)
            pieces.append(piece)
        halos.append(copies)
        loads[m].wait()
        swaps[m].wait_recv()

        @pl.when(q == 1)
        def _(m=m):
            passed[m].start()

        for n in range(end):
            if n != middle:
                packed[m][:, n * bs : (n + 1) * bs] = near[m][slot[m][middle - n]]
        for d in range(-REACH, REACH + 1):
            c = m + d + REACH
            panel[m + REACH, :, c * bs : (c + 1) * bs] = near[m][slot[m][d]]
        for copy in copies:
            copy.start()

    loads[half].wait()
    swaps[half].wait_recv()
    for m in range(half, rows):
        f = true_row(m, q) - (1 - q) * half
        for d in range(-REACH, REACH + 1):
            c = m + d + REACH
            if c < width:
                panel[m + REACH, :, c * bs : (c + 1) * bs] = far[f, slot[m][d]]

    tile = 2 * bs

    def span(c):
        return slice(c * tile, (c + 1) * tile)

    def product(left, row, n, low, high, c):
        a = left[row : row + n, :, low * bs : high * bs].reshape(n * bs, (high - low) * bs)
        b = panel[low:high, :, span(c)].reshape((high - low) * bs, tile)
        out = jnp.dot(a, b, preferred_element_type=jnp.float32)
        return out.reshape(n, bs, tile)

    def reached(p, c):
        return 2 * max(p, c - REACH // 2), 2 * min(p + REACH, c + REACH // 2) + 2

    def finish_square(m, c):
        for g in range(2):
            at = 2 * c + g
            d = at - REACH - m
            if -REACH <= d <= REACH:
                keep = jnp.where(slot[m][d] == slots, 0.0, 1.0).astype(jnp.float32)
                block = (total[m, :, at * bs : (at + 1) * bs] * keep).astype(jnp.bfloat16)
            else:
                block = zero
            square[m, :, at * bs : (at + 1) * bs] = block

    def finish_cube(m, c, value):
        for g in range(2):
            at = 2 * c + g
            whole = 3.0 * square[m, :, at * bs : (at + 1) * bs].astype(jnp.float32)
            whole = whole - 2.0 * value[:, g * bs : (g + 1) * bs]
            result[m, at] = whole.astype(jnp.bfloat16)

    sent = []

    def hand_out(m):
        i = true_row(m, q)
        for core in (1 - q, q):
            for s in range(own):
                block = result[m, home[m][core is q][s]]
                if core is q:
                    o_ref[i, s] = block
                else:
                    outbox[m, s] = block
        copy = pltpu.make_async_remote_copy(
            src_ref=outbox.at[m],
            dst_ref=o_ref.at[i],
            send_sem=osend_sem.at[m],
            recv_sem=orecv_sem.at[m],
            device_id=partner,
            device_id_type=MESH,
        )
        copy.start()
        sent.append((m, copy))

    def arrive(m):
        held[m].wait_recv()
        for copy in halos[m]:
            copy.wait_recv()

    for p in range(half // 2):
        for c in range(p, p + REACH + 1):
            low, high = reached(p, c)
            total[2 * p : 2 * p + 2, :, span(c)] = product(
                panel, 2 * p + REACH, 2, max(low, REACH), high, c
            )
    arrive(0)
    arrive(1)
    for p in (1, 0):
        for c in range(p, REACH):
            total[2 * p : 2 * p + 2, :, span(c)] += product(
                panel, 2 * p + REACH, 2, REACH - 2, REACH, c
            )
        if p:
            for c in range(p, p + REACH + 1):
                finish_square(2, c)
                finish_square(3, c)
            for c in range(p, p + REACH + 1):
                low, high = reached(p, c)
                value = product(square, 2, 2, low, high, c)
                finish_cube(2, c, value[0])
                finish_cube(3, c, value[1])
            hand_out(2)
            hand_out(3)
    arrive(2)
    for c in range(3):
        total[0:2, :, span(c)] += product(panel, REACH, 2, 1, 2, c)
    for c in range(REACH + 1):
        finish_square(1, c)
    for c in range(REACH + 1):
        low, high = reached(0, c)
        finish_cube(1, c, product(square, 1, 1, max(low, 1), high, c)[0])
    hand_out(1)
    for c in (3, 4):
        finish_square(0, c)
    for c in range(1, REACH + 1):
        part[:, span(c)] = product(square, 0, 1, 6, reached(0, c)[1], c)[0]
    arrive(3)
    for c in range(3):
        total[0:1, :, span(c)] += product(panel, REACH, 1, 0, 1, c)
        finish_square(0, c)
    for c in range(REACH + 1):
        value = product(square, 0, 1, reached(0, c)[0], 6, c)[0]
        if c:
            value = value + part[:, span(c)]
        finish_cube(0, c, value)
    hand_out(0)

    for copy in held + swaps + pieces:
        copy.wait_send()

    for m, copy in sent:
        copy.wait_send()
        pltpu.make_async_remote_copy(
            src_ref=outbox.at[m],
            dst_ref=o_ref.at[true_row(m, 1 - q)],
            send_sem=osend_sem.at[m],
            recv_sem=orecv_sem.at[m],
            device_id=partner,
            device_id_type=MESH,
        ).wait_recv()


def local(matrix, columns):
    rows, own, bs = matrix.shape[0], matrix.shape[1], matrix.shape[2]
    slots = columns.shape[1]
    half = rows // 2
    assert rows == 2 * REACH and lax.axis_size("col") == 2
    width = rows + REACH
    kind = matrix.dtype
    dma = pltpu.SemaphoreType.DMA
    return pl.pallas_call(
        functools.partial(kernel, rows, slots, bs),
        out_shape=jax.ShapeDtypeStruct(matrix.shape, kind),
        in_specs=[
            pl.BlockSpec(memory_space=pltpu.HBM),
            pl.BlockSpec(memory_space=pltpu.HBM),
        ],
        out_specs=pl.BlockSpec(memory_space=pltpu.VMEM),
        scratch_shapes=[pltpu.VMEM((slots + 1, bs, bs), kind)] * half
        + [pltpu.VMEM((rows - half, slots + 1, bs, bs), kind)]
        + [pltpu.VMEM((bs, (rows - m) * bs), kind) for m in range(half)]
        + [
            pltpu.VMEM((width, bs, width * bs), kind),
            pltpu.VMEM((half, bs, width * bs), kind),
            pltpu.VMEM((half, bs, width * bs), jnp.float32),
            pltpu.VMEM((bs, width * bs), jnp.float32),
            pltpu.VMEM((half, width + 1, bs, bs), kind),
            pltpu.VMEM((half, own, bs, bs), kind),
            pltpu.SMEM(columns.shape, columns.dtype),
            dma((half + 1,)),
            dma,
            dma((half + 1,)),
            dma((half + 1,)),
            dma((half,)),
            dma((half,)),
            dma((2 * half - 1,)),
            dma((2 * half - 1,)),
            dma((half,)),
            dma((half,)),
        ],
        compiler_params=pltpu.CompilerParams(
            collective_id=0, has_side_effects=True, vmem_limit_bytes=40 * 1024 * 1024
        ),
    )(
        pltpu.with_memory_space_constraint(columns, pltpu.HBM),
        pltpu.with_memory_space_constraint(matrix, pltpu.HBM),
    )


def solution(mesh):
    placed = (P(("geom", "row"), "col", None, None), P("row", None))
    return jax.shard_map(
        local,
        mesh=mesh,
        in_specs=placed,
        out_specs=P(("geom", "row"), "col", None, None),
        check_vma=False,
    )
```

```python
import functools

import jax
import jax.numpy as jnp
from jax import lax
from jax.experimental import pallas as pl
from jax.experimental.pallas import tpu as pltpu
from jax.sharding import PartitionSpec as P

REACH = 4
MESH = pl.DeviceIdType.MESH


def kernel(
    rows, slots, bs,
    cols_hbm, x_ref, o_ref,
    near0, near1, near2, near3, far, send0, send1, send2, send3, panel, square, total, part, result,
    outbox, cols_ref,
    local_sem, cols_sem, xsend_sem, xrecv_sem, dsend_sem, drecv_sem, hsend_sem, hrecv_sem, osend_sem, orecv_sem, met_sem,
):
    half = rows // 2
    own = x_ref.shape[1]
    width = rows + REACH
    near = (near0, near1, near2, near3)
    packed = (send0, send1, send2, send3)
    q = lax.axis_index("col")
    r = lax.axis_index("row")
    devices = lax.axis_size("row")
    count = rows * devices
    sign = 1 - 2 * q
    facing = lax.rem(r + 2 * q - 1 + devices, devices)
    partner = {"col": 1 - q}
    neighbour = {"row": facing, "col": 1 - q}

    def true_row(m, core):
        return m + core * (rows - 1 - 2 * m)

    barrier = pltpu.get_barrier_semaphore()

    @pl.when(q == 1)
    def _():
        pl.semaphore_signal(barrier, inc=1, device_id=neighbour, device_id_type=MESH)

    pl.semaphore_signal(barrier, inc=1, device_id=partner, device_id_type=MESH)

    table = pltpu.make_async_copy(cols_hbm, cols_ref, cols_sem)
    table.start()
    mine = pl.ds(q * own, own)
    loads = []
    for m in range(half):
        loads.append(
            pltpu.make_async_copy(x_ref.at[true_row(m, q)], near[m].at[mine], local_sem.at[m])
        )
    loads.append(
        pltpu.make_async_copy(
            x_ref.at[pl.ds((1 - q) * half, half)], far.at[:, mine], local_sem.at[half]
        )
    )
    for copy in loads:
        copy.start()

    def diagonal(m, source):
        at = REACH - 1 - m
        return pltpu.make_async_remote_copy(
            src_ref=source,
            dst_ref=panel.at[at, :, pl.ds(at * bs, bs)],
            send_sem=dsend_sem.at[m],
            recv_sem=drecv_sem.at[m],
            device_id=neighbour,
            device_id_type=MESH,
        )

    held = [diagonal(m, x_ref.at[true_row(m, 0), 0]) for m in range(half)]
    passed = [diagonal(m, near[m].at[0]) for m in range(half)]

    swaps = []
    for m in range(half):
        swaps.append(
            pltpu.make_async_remote_copy(
                src_ref=x_ref.at[true_row(m, 1 - q)],
                dst_ref=near[m].at[mine],
                send_sem=xsend_sem.at[m],
                recv_sem=xrecv_sem.at[m],
                device_id=partner,
                device_id_type=MESH,
            )
        )
    swaps.append(
        pltpu.make_async_remote_copy(
            src_ref=x_ref.at[pl.ds(q * half, half)],
            dst_ref=far.at[:, mine],
            send_sem=xsend_sem.at[half],
            recv_sem=xrecv_sem.at[half],
            device_id=partner,
            device_id_type=MESH,
        )
    )

    zero = jnp.zeros((bs, bs), x_ref.dtype)
    for m in range(half):
        near[m][slots] = zero
    for f in range(rows - half):
        far[f, slots] = zero
    for m in range(half):
        result[m, width] = zero
    for j in range(width):
        m = j - REACH
        if m < 0:
            blank = range(rows + 1 + m, width)
        else:
            blank = [c for c in range(width) if not m <= c <= m + 2 * REACH]
        for c in blank:
            panel[j, :, c * bs : (c + 1) * bs] = zero

    pl.semaphore_wait(barrier, 2 - q)

    @pl.when(q == 0)
    def _():
        pl.semaphore_signal(met_sem, inc=1, device_id=neighbour, device_id_type=MESH)

    for copy in swaps[:half]:
        copy.start()

    @pl.when(q == 0)
    def _():
        for copy in held:
            copy.start()

    swaps[half].start()
    table.wait()

    def offset_of(i, k):
        col = cols_ref[i, k]
        d = col - (r * rows + i)
        d = jnp.where(d > count // 2, d - count, d)
        d = jnp.where(d < -(count // 2), d + count, d)
        return jnp.where(col >= 0, d * sign, 2 * count)

    offset = [[offset_of(true_row(m, q), k) for k in range(slots)] for m in range(rows)]

    def slot_of(m, d):
        found = jnp.int32(slots)
        for k in range(slots):
            found = jnp.where(offset[m][k] == d, k, found)
        return found

    slot = [{d: slot_of(m, d) for d in range(-REACH, REACH + 1)} for m in range(rows)]

    def home_of(m, k):
        d = offset_of(true_row(m, q), k)
        return jnp.where((d >= -REACH) & (d <= REACH), d + (m + REACH), width)

    home = [
        [[home_of(m, core * own + s) for s in range(own)] for core in (1 - q, q)]
        for m in range(half)
    ]

    halos, pieces = [], []
    for m in range(half):
        middle, end = REACH - 1 - m, rows - m
        spans = [(middle + 1, end)] + ([(0, middle)] if middle else [])
        copies = []
        for low, high in spans:
            at = len(pieces)
            piece = pltpu.make_async_remote_copy(
                src_ref=packed[m].at[:, pl.ds(low * bs, (high - low) * bs)],
                dst_ref=panel.at[middle, :, pl.ds(low * bs, (high - low) * bs)],
                send_sem=hsend_sem.at[at],
                recv_sem=hrecv_sem.at[at],
                device_id=neighbour,
                device_id_type=MESH,
            )
            copies.append(piece)
            pieces.append(piece)
        halos.append(copies)
        loads[m].wait()
        swaps[m].wait_recv()

        @pl.when(q == 1)
        def _(m=m):
            if m == 0:
                pl.semaphore_wait(met_sem, 1)
            passed[m].start()

        for n in range(end):
            if n != middle:
                packed[m][:, n * bs : (n + 1) * bs] = near[m][slot[m][middle - n]]
        for d in range(-REACH, REACH + 1):
            c = m + d + REACH
            panel[m + REACH, :, c * bs : (c + 1) * bs] = near[m][slot[m][d]]
        for copy in copies:
            copy.start()

    loads[half].wait()
    swaps[half].wait_recv()
    for m in range(half, rows):
        f = true_row(m, q) - (1 - q) * half
        for d in range(-REACH, REACH + 1):
            c = m + d + REACH
            if c < width:
                panel[m + REACH, :, c * bs : (c + 1) * bs] = far[f, slot[m][d]]

    tile = 2 * bs

    def span(c):
        return slice(c * tile, (c + 1) * tile)

    def product(left, row, n, low, high, c):
        a = left[row : row + n, :, low * bs : high * bs].reshape(n * bs, (high - low) * bs)
        b = panel[low:high, :, span(c)].reshape((high - low) * bs, tile)
        out = jnp.dot(a, b, preferred_element_type=jnp.float32)
        return out.reshape(n, bs, tile)

    def reached(p, c):
        return 2 * max(p, c - REACH // 2), 2 * min(p + REACH, c + REACH // 2) + 2

    def finish_square(m, c):
        for g in range(2):
            at = 2 * c + g
            d = at - REACH - m
            if -REACH <= d <= REACH:
                keep = jnp.where(slot[m][d] == slots, 0.0, 1.0).astype(jnp.float32)
                block = (total[m, :, at * bs : (at + 1) * bs] * keep).astype(jnp.bfloat16)
            else:
                block = zero
            square[m, :, at * bs : (at + 1) * bs] = block

    def finish_cube(m, c, value):
        for g in range(2):
            at = 2 * c + g
            whole = 3.0 * square[m, :, at * bs : (at + 1) * bs].astype(jnp.float32)
            whole = whole - 2.0 * value[:, g * bs : (g + 1) * bs]
            result[m, at] = whole.astype(jnp.bfloat16)

    sent = []

    def hand_out(m):
        i = true_row(m, q)
        for core in (1 - q, q):
            for s in range(own):
                block = result[m, home[m][core is q][s]]
                if core is q:
                    o_ref[i, s] = block
                else:
                    outbox[m, s] = block
        copy = pltpu.make_async_remote_copy(
            src_ref=outbox.at[m],
            dst_ref=o_ref.at[i],
            send_sem=osend_sem.at[m],
            recv_sem=orecv_sem.at[m],
            device_id=partner,
            device_id_type=MESH,
        )
        copy.start()
        sent.append((m, copy))

    def arrive(m):
        held[m].wait_recv()
        for copy in halos[m]:
            copy.wait_recv()

    for p in range(half // 2):
        for c in range(p, p + REACH + 1):
            low, high = reached(p, c)
            total[2 * p : 2 * p + 2, :, span(c)] = product(
                panel, 2 * p + REACH, 2, max(low, REACH), high, c
            )
    arrive(0)
    arrive(1)
    for p in (1, 0):
        for c in range(p, REACH):
            total[2 * p : 2 * p + 2, :, span(c)] += product(
                panel, 2 * p + REACH, 2, REACH - 2, REACH, c
            )
        if p:
            for c in range(p, p + REACH + 1):
                finish_square(2, c)
                finish_square(3, c)
            for c in range(p, p + REACH + 1):
                low, high = reached(p, c)
                value = product(square, 2, 2, low, high, c)
                finish_cube(2, c, value[0])
                finish_cube(3, c, value[1])
            hand_out(2)
            hand_out(3)
    arrive(2)
    for c in range(3):
        total[0:2, :, span(c)] += product(panel, REACH, 2, 1, 2, c)
    for c in range(REACH + 1):
        finish_square(1, c)
    for c in range(REACH + 1):
        low, high = reached(0, c)
        finish_cube(1, c, product(square, 1, 1, max(low, 1), high, c)[0])
    hand_out(1)
    for c in (3, 4):
        finish_square(0, c)
    for c in range(1, REACH + 1):
        part[:, span(c)] = product(square, 0, 1, 6, reached(0, c)[1], c)[0]
    arrive(3)
    for c in range(3):
        total[0:1, :, span(c)] += product(panel, REACH, 1, 0, 1, c)
        finish_square(0, c)
    for c in range(REACH + 1):
        value = product(square, 0, 1, reached(0, c)[0], 6, c)[0]
        if c:
            value = value + part[:, span(c)]
        finish_cube(0, c, value)
    hand_out(0)

    for copy in held + swaps + pieces:
        copy.wait_send()

    for m, copy in sent:
        copy.wait_send()
        pltpu.make_async_remote_copy(
            src_ref=outbox.at[m],
            dst_ref=o_ref.at[true_row(m, 1 - q)],
            send_sem=osend_sem.at[m],
            recv_sem=orecv_sem.at[m],
            device_id=partner,
            device_id_type=MESH,
        ).wait_recv()


def local(matrix, columns):
    rows, own, bs = matrix.shape[0], matrix.shape[1], matrix.shape[2]
    slots = columns.shape[1]
    half = rows // 2
    assert rows == 2 * REACH and lax.axis_size("col") == 2
    width = rows + REACH
    kind = matrix.dtype
    dma = pltpu.SemaphoreType.DMA
    return pl.pallas_call(
        functools.partial(kernel, rows, slots, bs),
        out_shape=jax.ShapeDtypeStruct(matrix.shape, kind),
        in_specs=[
            pl.BlockSpec(memory_space=pltpu.HBM),
            pl.BlockSpec(memory_space=pltpu.HBM),
        ],
        out_specs=pl.BlockSpec(memory_space=pltpu.VMEM),
        scratch_shapes=[pltpu.VMEM((slots + 1, bs, bs), kind)] * half
        + [pltpu.VMEM((rows - half, slots + 1, bs, bs), kind)]
        + [pltpu.VMEM((bs, (rows - m) * bs), kind) for m in range(half)]
        + [
            pltpu.VMEM((width, bs, width * bs), kind),
            pltpu.VMEM((half, bs, width * bs), kind),
            pltpu.VMEM((half, bs, width * bs), jnp.float32),
            pltpu.VMEM((bs, width * bs), jnp.float32),
            pltpu.VMEM((half, width + 1, bs, bs), kind),
            pltpu.VMEM((half, own, bs, bs), kind),
            pltpu.SMEM(columns.shape, columns.dtype),
            dma((half + 1,)),
            dma,
            dma((half + 1,)),
            dma((half + 1,)),
            dma((half,)),
            dma((half,)),
            dma((2 * half - 1,)),
            dma((2 * half - 1,)),
            dma((half,)),
            dma((half,)),
            pltpu.SemaphoreType.REGULAR,
        ],
        compiler_params=pltpu.CompilerParams(
            collective_id=0, has_side_effects=True, vmem_limit_bytes=40 * 1024 * 1024
        ),
    )(
        pltpu.with_memory_space_constraint(columns, pltpu.HBM),
        pltpu.with_memory_space_constraint(matrix, pltpu.HBM),
    )


def solution(mesh):
    placed = (P(("geom", "row"), "col", None, None), P("row", None))
    return jax.shard_map(
        local,
        mesh=mesh,
        in_specs=placed,
        out_specs=P(("geom", "row"), "col", None, None),
        check_vma=False,
    )
```
